32 devices in a mesh: expert: 4 (over y, core), dp: 8 (over z, x).
Axes of the slice: x: 2, y: 2, z: 4, core: 2. Of those that a mesh axis runs over, the one named last changes fastest.
Arguments:
- tokens: bfloat16 [32768, 2048], P(('expert', 'dp')), may hold values from -6 to 6
- block_expert: int32 [256, 1], P(('expert', 'dp')), may hold values from 0 to 3; in each aligned block of 8 rows (0 to 7, 8 to 15, ...) at most 4 rows name the same one
- gate_weight: bfloat16 [4, 2048, 768], P('expert', 'dp'), may hold values from -0.125 to 0.125
- up_weight: bfloat16 [4, 2048, 768], P('expert', 'dp'), may hold values from -0.125 to 0.125
- down_weight: bfloat16 [4, 768, 2048], P('expert', None, 'dp'), may hold values from -0.21875 to 0.21875
Outputs:
- r_factor: float32 [4, 768, 768], P('expert', 'dp')
- compressed_down: float32 [4, 768, 2048], P('expert', None, 'dp')
The draws below stay inside these ranges and needn't reach their ends.
Inputs may be any that keep to these rules, and one draw needn't show every extreme that they name: `block_expert`: among the 8 blocks of one device, at most 4 name the same expert, and in every draw some device has exactly 4 blocks for one expert.
All inputs are finite; a program needn't handle non-finite values.
Results may differ from the reference program's by a relative error of at most 0.0003.
Values may be sent and summed in bfloat16 or wider, within the bound.
No kernel may reach another device: no remote copies, remote signals or barrier semaphores. Data moves between devices by JAX's collectives and lax.ppermute only.
A program may use at most 128 MiB of HBM per device.

```python
import math
import jax
import jax.numpy as jnp
import numpy as np
from jax import lax

D = 2048
FF = 768
BROWS = 128
BLK_DEV = 8
EXPERTS = 4
CAP = 4
NBLK = 256
TOKENS = 32768
ROWS_AVG = 8192


def steps_of(own_key, shape, shards, least, largest):
    def one(dim, blocks):
        heights = jax.random.uniform(jax.random.fold_in(jax.random.fold_in(own_key, 6), dim), (blocks,), jnp.float32, least / len(shards), largest / len(shards))
        return jnp.repeat(jnp.exp(heights), shape[dim] // blocks).reshape((-1,) + (1,) * (len(shape) - dim - 1))

    level = one(*shards[0])
    for cut in shards[1:]:
        level = level * one(*cut)
    return level


def assign_block(stream_key, own, number, rows, amount, top, reach, lean):
    ranking = jax.random.permutation(stream_key, amount)
    crowded, usual = portions_of(amount, rows * top, reach, lean, True), portions_of(amount, rows * top, reach, lean, False)
    places = jnp.arange(amount)

    def named(tallies, rotation):
        used = int((tallies > 0).sum())
        fixed = max(1, used // 4)
        passed = fixed + (places - fixed + rotation * (used - fixed)) % max(1, amount - fixed)
        return jnp.zeros((amount,), jnp.int32).at[ranking[jnp.where(places < fixed, places, passed)]].set(jnp.asarray(tallies, jnp.int32))

    tallies = jnp.where(number % 4 == 0, named(crowded, number // 4), named(usual, number - number // 4 - 1))
    mixed = jax.random.permutation(jax.random.fold_in(own, 3), amount)
    donor, sink = mixed[0:amount // 2 * 2:2], mixed[1:amount // 2 * 2:2]
    margin = jnp.minimum(tallies[donor] - 1, reach - tallies[sink]) // 2
    margin = jnp.where((donor == ranking[0]) | (sink == ranking[0]) | (tallies[sink] == 0), 0, jnp.maximum(margin, 0))
    passed = jax.random.randint(jax.random.fold_in(own, 4), (amount // 2,), 0, 1 << 20) % (margin + 1)
    tallies = tallies.at[donor].add(-passed).at[sink].add(passed)
    members = jnp.searchsorted(jnp.cumsum(tallies), jnp.arange(rows * top), side="right").astype(jnp.int32)
    listing = members.reshape(top, rows).T
    listing = listing[jax.random.permutation(jax.random.fold_in(own, 1), rows)]
    rotation = jax.random.randint(jax.random.fold_in(own, 2), (rows, 1), 0, top)
    return jnp.take_along_axis(listing, (jnp.arange(top)[None, :] + rotation) % top, axis=1)


def portions_of(number_of, total, reach, slope, full):
    loads = [(1 << 20) // math.isqrt(standing ** slope) + 1 for standing in range(1, number_of + 1)]
    largest = reach if full else min(reach, max(-(-total // number_of), total * loads[0] // sum(loads)))
    least = 1 if total - largest >= number_of - 1 else 0
    counts, surplus = [largest] + [least] * (number_of - 1), total - largest - least * (number_of - 1)
    while surplus > 0:
        movable = [i for i in range(1, number_of) if counts[i] < largest] or [i for i in range(1, number_of) if counts[i] < reach]
        mass, left = sum([loads[i] for i in movable]), surplus
        for i in movable:
            extra = min(reach - counts[i], max(1, left * loads[i] // mass), surplus)
            counts[i] = counts[i] + extra
            surplus = surplus - extra
    return np.array(counts)


def gaussian(own_key, shape, scale, reach, pieces=(), held_as=jnp.bfloat16):
    gain = steps_of(own_key, shape, pieces, -0.22, 0.18) if pieces else 1.0
    entries = jax.random.normal(own_key, shape, jnp.float32) * scale * gain
    return jnp.minimum(jnp.maximum(entries, -reach), reach).astype(held_as)


def setup_inputs(seed: int = 0) -> dict:
    streams_of = jax.random.split(jax.random.key(seed), 6)
    tokens = gaussian(streams_of[0], (TOKENS, D), 1.0, 6.0, ((0, 32),))
    block_expert_keys = jax.random.split(jax.random.fold_in(streams_of[1], 1), NBLK // BLK_DEV)
    block_expert_turns = jax.random.permutation(jax.random.fold_in(streams_of[1], 3), NBLK // BLK_DEV)
    block_expert = jax.vmap(lambda own, number: assign_block(jax.random.fold_in(streams_of[1], 2), own, number, BLK_DEV, EXPERTS, 1, CAP, 2))(block_expert_keys, block_expert_turns).reshape((NBLK, 1))
    gate_weight = gaussian(streams_of[2], (EXPERTS, D, FF), D ** -0.5, 0.125, ((0, 4), (1, 8)))
    up_weight = gaussian(streams_of[3], (EXPERTS, D, FF), D ** -0.5, 0.125, ((0, 4), (1, 8)))
    down_weight = gaussian(streams_of[4], (EXPERTS, FF, D), FF ** -0.5, 0.21875, ((0, 4), (2, 8)))
    return dict(tokens=tokens, block_expert=block_expert, gate_weight=gate_weight, up_weight=up_weight, down_weight=down_weight)


damping = 0.05

def reference(tokens, block_expert, gate_weight, up_weight, down_weight):
    blocks = tokens.reshape(NBLK, BROWS, D)
    ids = block_expert[:, 0].astype(jnp.int32)

    def step(gram, item):
        block, expert_id = item
        gate = jnp.dot(block.astype(jnp.float32), gate_weight[expert_id].astype(jnp.float32), preferred_element_type=jnp.float32)
        upper_part = jnp.dot(block.astype(jnp.float32), up_weight[expert_id].astype(jnp.float32), preferred_element_type=jnp.float32)
        hidden = jax.nn.silu(gate) * upper_part
        term = jnp.dot(hidden.T, hidden, precision=lax.Precision.HIGHEST)
        return (gram.at[expert_id].add(term), None)
    gram, _ = lax.scan(step, jnp.zeros((EXPERTS, FF, FF), jnp.float32), (blocks, ids))
    gram = gram / float(ROWS_AVG) + damping * jnp.eye(FF, dtype=jnp.float32)[None]
    lower = jnp.linalg.cholesky(gram)
    r_factor = jnp.transpose(lower, (0, 2, 1))
    compressed = jnp.einsum('eij,ejk->eik', r_factor, down_weight.astype(jnp.float32), precision=lax.Precision.HIGHEST)
    return (r_factor, compressed)
```

```python
import functools
import jax
import jax.numpy as jnp
from jax import lax
from jax.experimental import pallas as pl
from jax.experimental.pallas import tpu as pltpu
from jax.sharding import PartitionSpec as P

BROWS = 128
NB = 128
PIVOTS = 8
HIGHEST = lax.Precision.HIGHEST


damping = 0.05


def factor_block(rows):
    q = PIVOTS
    groups = NB // 8
    left = list(rows)
    lane = lax.broadcasted_iota(jnp.int32, (8, NB), 1)
    sub = lax.broadcasted_iota(jnp.int32, (8, NB), 0)
    right = [jnp.where(lane == sub + 8 * g, 1.0, 0.0).astype(jnp.float32) for g in range(groups)]

    def spread(x):
        return jnp.broadcast_to(x, (8, NB))

    for t in range(NB // q):
        j0 = t * q
        g, s0 = j0 // 8, j0 % 8
        p1, p2 = left[g], right[g]
        a = {}
        for i in range(q):
            for k in range(i, q):
                a[i, k] = spread(p1[s0 + i : s0 + i + 1, j0 + k : j0 + k + 1])
        r1 = [spread(p1[s0 + i : s0 + i + 1, :]) for i in range(q)]
        r2 = [spread(p2[s0 + i : s0 + i + 1, :]) for i in range(q)]
        inv, rs = [], []
        for c in range(q):
            root = lax.rsqrt(a[c, c])
            rs.append(root)
            inv.append(root * root)
            for i in range(c + 1, q):
                m = a[c, i] * inv[c]
                for k in range(i, q):
                    a[i, k] = a[i, k] - m * a[c, k]
                r1[i] = r1[i] - m * r1[c]
                r2[i] = r2[i] - m * r2[c]
        for below in range(g, groups):
            if below == g and s0 + q == 8:
                continue
            x1, x2 = left[below], right[below]
            cols = [spread(x1[:, j0 + c : j0 + c + 1]) for c in range(q)]
            for c in range(q):
                tc = cols[c] * inv[c]
                for k in range(c + 1, q):
                    cols[k] = cols[k] - tc * a[c, k]
                if below == g:
                    tc = jnp.where(sub >= s0 + q, tc, 0.0)
                x1 = x1 - tc * r1[c]
                x2 = x2 - tc * r2[c]
            left[below], right[below] = x1, x2
        x1, x2 = left[g], right[g]
        for c in range(q):
            x1 = jnp.where(sub == s0 + c, r1[c] * rs[c], x1)
            x2 = jnp.where(sub == s0 + c, r2[c] * rs[c], x2)
        left[g], right[g] = x1, x2
    return left, right


def split3(x):
    first = x.astype(jnp.bfloat16)
    rest = x - first.astype(jnp.float32)
    second = rest.astype(jnp.bfloat16)
    third = (rest - second.astype(jnp.float32)).astype(jnp.bfloat16)
    return first, second, third


def factor_kernel(place_ref, gram_ref, down_ref, mine_ref, product_ref, work, inverse):
    width = gram_ref.shape[0]
    my_rows = mine_ref.shape[0]
    count = width // NB
    work[...] = gram_ref[...]
    sub = lax.broadcasted_iota(jnp.int32, (8, NB), 0)
    lane = lax.broadcasted_iota(jnp.int32, (8, NB), 1)

    def step(kb, carry):
        off = pl.multiple_of(kb * NB, NB)
        rows = [work[pl.ds(off + 8 * i, 8), pl.ds(off, NB)] for i in range(NB // 8)]
        upper, low_inv = factor_block(rows)
        for i in range(NB // 8):
            work[pl.ds(off + 8 * i, 8), pl.ds(off, NB)] = jnp.where(lane >= sub + 8 * i, upper[i], 0.0)
            inverse[8 * i : 8 * i + 8, :] = low_inv[i]
        for k in range(count):
            @pl.when(kb == k)
            def _():
                at, lo = k * NB, (k + 1) * NB
                if k < count - 1:
                    panel = jnp.dot(
                        inverse[...], work[at:lo, lo:], precision=HIGHEST, preferred_element_type=jnp.float32
                    )
                    work[at:lo, lo:] = panel
                    work[lo:, at:lo] = jnp.zeros((width - lo, NB), jnp.float32)
                    for i in range(k + 1, count):
                        a = i * NB
                        work[a : a + NB, a:] -= lax.dot_general(
                            panel[:, a - lo : a - lo + NB],
                            panel[:, a - lo :],
                            (((0,), (0,)), ((), ())),
                            precision=HIGHEST,
                            preferred_element_type=jnp.float32,
                        )
                down = down_ref[at:, :]
                parts = [
                    jnp.dot(piece, down, preferred_element_type=jnp.float32)
                    for piece in split3(work[at:lo, at:])
                ]
                product_ref[at:lo, :] = parts[0] + (parts[1] + parts[2])
        return carry

    lax.fori_loop(0, count, step, 0)
    start = pl.multiple_of(place_ref[0] * my_rows, 8)
    mine_ref[...] = work[pl.ds(start, my_rows), :]


def factor_and_product(gram, down, place, my_rows):
    width = gram.shape[0]
    vmem = pl.BlockSpec(memory_space=pltpu.VMEM)
    return pl.pallas_call(
        factor_kernel,
        out_shape=(
            jax.ShapeDtypeStruct((my_rows, width), jnp.float32),
            jax.ShapeDtypeStruct((width, down.shape[1]), jnp.float32),
        ),
        in_specs=[pl.BlockSpec(memory_space=pltpu.SMEM), vmem, vmem],
        out_specs=(vmem, vmem),
        scratch_shapes=[pltpu.VMEM((width, width), jnp.float32), pltpu.VMEM((NB, NB), jnp.float32)],
        name="factor",
    )(place, gram, down)


def on_device(tokens, block_expert, gate_weight, up_weight, down_weight):
    n_expert = lax.axis_size("expert")
    n_data = lax.axis_size("dp")
    exp_local = gate_weight.shape[0]
    width = gate_weight.shape[2]
    model = tokens.shape[1]
    experts = exp_local * n_expert
    blk_count = block_expert.shape[0]
    capacity = max(2, 2 * blk_count // experts)
    rows_avg = blk_count * BROWS * n_data * n_expert // experts
    blocks = tokens.reshape(blk_count, BROWS, model)
    ids = block_expert[:, 0]
    positions = jnp.arange(blk_count, dtype=jnp.int32)
    same = ids[:, None] == ids[None, :]
    earlier = positions[None, :] < positions[:, None]
    ranks = jnp.sum((same & earlier).astype(jnp.int32), axis=1)
    slots = jnp.arange(experts * capacity, dtype=jnp.int32)
    match = (ids[None, :] == (slots // capacity)[:, None]) & (
        ranks[None, :] == (slots % capacity)[:, None]
    )
    found = jnp.sum(match.astype(jnp.int32), axis=1)
    source = jnp.sum(match.astype(jnp.int32) * positions[None, :], axis=1) + (1 - found) * blk_count
    padded = jnp.concatenate([blocks, jnp.zeros((1, BROWS, model), jnp.bfloat16)], axis=0)
    outgoing = padded[source].reshape(n_expert, exp_local, capacity, BROWS, model)
    arrived = lax.all_to_all(outgoing, "expert", split_axis=0, concat_axis=0, tiled=True)
    eye = jnp.eye(width, dtype=jnp.float32)
    my_rows = width // n_data
    rows = arrived[:, 0].reshape(-1, model)
    gate = jnp.dot(
        rows,
        lax.all_gather(gate_weight[0], "dp", axis=0, tiled=True),
        preferred_element_type=jnp.float32,
    )
    lifted = jnp.dot(
        rows,
        lax.all_gather(up_weight[0], "dp", axis=0, tiled=True),
        preferred_element_type=jnp.float32,
    )
    hidden = jax.nn.silu(gate) * lifted
    gram = jnp.dot(hidden.T, hidden, precision=lax.Precision.HIGHEST) / float(rows_avg)
    total = lax.psum(gram, "dp") + damping * eye
    place = jnp.reshape(lax.axis_index("dp"), (1,)).astype(jnp.int32)
    mine, product = factor_and_product(total, down_weight[0], place, my_rows)
    return (mine[None], product[None])


def solution(mesh):
    placed = (
        P(("expert", "dp"), None),
        P(("expert", "dp"), None),
        P("expert", "dp", None),
        P("expert", "dp", None),
        P("expert", None, "dp"),
    )
    return jax.shard_map(
        on_device,
        mesh=mesh,
        in_specs=placed,
        out_specs=(P("expert", "dp", None), P("expert", None, "dp")),
        check_vma=False,
    )
```

```python
import functools
import jax
import jax.numpy as jnp
from jax import lax
from jax.experimental import pallas as pl
from jax.experimental.pallas import tpu as pltpu
from jax.sharding import PartitionSpec as P

BROWS = 128
NB = 128
PIVOTS = 8
HIGHEST = lax.Precision.HIGHEST


damping = 0.05


def factor_block(rows):
    q = PIVOTS
    groups = NB // 8
    left = list(rows)
    lane = lax.broadcasted_iota(jnp.int32, (8, NB), 1)
    sub = lax.broadcasted_iota(jnp.int32, (8, NB), 0)
    right = [jnp.where(lane == sub + 8 * g, 1.0, 0.0).astype(jnp.float32) for g in range(groups)]

    def spread(x):
        return jnp.broadcast_to(x, (8, NB))

    for t in range(NB // q):
        j0 = t * q
        g, s0 = j0 // 8, j0 % 8
        p1, p2 = left[g], right[g]
        a = {}
        for i in range(q):
            for k in range(i, q):
                a[i, k] = spread(p1[s0 + i : s0 + i + 1, j0 + k : j0 + k + 1])
        r1 = [spread(p1[s0 + i : s0 + i + 1, :]) for i in range(q)]
        r2 = [spread(p2[s0 + i : s0 + i + 1, :]) for i in range(q)]
        inv, rs = [], []
        for c in range(q):
            root = lax.rsqrt(a[c, c])
            rs.append(root)
            inv.append(root * root)
            for i in range(c + 1, q):
                m = a[c, i] * inv[c]
                for k in range(i, q):
                    a[i, k] = a[i, k] - m * a[c, k]
                r1[i] = r1[i] - m * r1[c]
                r2[i] = r2[i] - m * r2[c]
        for below in range(g, groups):
            if below == g and s0 + q == 8:
                continue
            x1, x2 = left[below], right[below]
            cols = [spread(x1[:, j0 + c : j0 + c + 1]) for c in range(q)]
            for c in range(q):
                tc = cols[c] * inv[c]
                for k in range(c + 1, q):
                    cols[k] = cols[k] - tc * a[c, k]
                if below == g:
                    tc = jnp.where(sub >= s0 + q, tc, 0.0)
                x1 = x1 - tc * r1[c]
                x2 = x2 - tc * r2[c]
            left[below], right[below] = x1, x2
        x1, x2 = left[g], right[g]
        for c in range(q):
            x1 = jnp.where(sub == s0 + c, r1[c] * rs[c], x1)
            x2 = jnp.where(sub == s0 + c, r2[c] * rs[c], x2)
        left[g], right[g] = x1, x2
    return left, right


def split3(x):
    first = x.astype(jnp.bfloat16)
    rest = x - first.astype(jnp.float32)
    second = rest.astype(jnp.bfloat16)
    third = (rest - second.astype(jnp.float32)).astype(jnp.bfloat16)
    return first, second, third


def dispatch_kernel(slots, me_ref, ids_ref, tokens_ref, *rest):
    outs, (held, in_sem, out_sem) = rest[: len(slots)], rest[len(slots) :]
    blocks = held.shape[0] - 1
    rows = held.shape[1]
    loads = [
        pltpu.make_async_copy(tokens_ref.at[pl.ds(b * rows, rows), :], held.at[b], in_sem.at[b]) for b in range(blocks)
    ]
    for load in loads:
        load.start()
    held[blocks] = jnp.zeros(held.shape[1:], held.dtype)
    ids = [ids_ref[b, 0] for b in range(blocks)]
    picks = {}
    for offset in sorted({offset for offset, _, _ in slots}):
        expert = me_ref[0] ^ offset
        deepest = max(first + count for other, first, count in slots if other == offset)
        rank = jnp.int32(0)
        chosen = [jnp.int32(blocks)] * deepest
        for b in range(blocks):
            same = ids[b] == expert
            for s in range(deepest):
                chosen[s] = jnp.where(same & (rank == s), b, chosen[s])
            rank = rank + same.astype(jnp.int32)
        picks[offset] = chosen
    for load in loads:
        load.wait()
    stores = []
    for out, (offset, first, count) in zip(outs, slots):
        for s in range(count):
            stores.append(
                pltpu.make_async_copy(
                    held.at[picks[offset][first + s]], out.at[pl.ds(s * rows, rows), :], out_sem.at[len(stores)]
                )
            )
            stores[-1].start()
    for store in stores:
        store.wait()


def dispatch(tokens, ids, me, slots):
    blocks = ids.shape[0]
    rows, model = tokens.shape[0] // blocks, tokens.shape[1]
    anywhere = pl.BlockSpec(memory_space=pl.ANY)
    smem = pl.BlockSpec(memory_space=pltpu.SMEM)
    total = sum(count for _, _, count in slots)
    return pl.pallas_call(
        functools.partial(dispatch_kernel, slots),
        out_shape=[jax.ShapeDtypeStruct((count * rows, model), tokens.dtype) for _, _, count in slots],
        in_specs=[smem, smem, anywhere],
        out_specs=[anywhere] * len(slots),
        scratch_shapes=[
            pltpu.VMEM((blocks + 1, rows, model), tokens.dtype),
            pltpu.SemaphoreType.DMA((blocks,)),
            pltpu.SemaphoreType.DMA((total,)),
        ],
        cost_estimate=pl.CostEstimate(flops=0, bytes_accessed=2 * tokens.size * 2, transcendentals=0),
        name="dispatch",
    )(me, ids, tokens)


def upper_blocks(width):
    count = width // NB
    place, at = {}, 0
    for i in range(count):
        for j in range(i, count):
            place[i, j] = at
            at += 1
    return place


def add_gram(acc, hidden):
    width = hidden.shape[1]
    place = upper_blocks(width)
    high = hidden.astype(jnp.bfloat16)
    low = (hidden - high.astype(jnp.float32)).astype(jnp.bfloat16)
    one = jnp.concatenate([high, high, low], axis=0)
    two = jnp.concatenate([high, low, high], axis=0)
    wide = 2 * NB
    for a in range(0, width, wide):
        piece = lax.dot_general(
            one[:, a : a + wide], two[:, a:], (((0,), (0,)), ((), ())), preferred_element_type=jnp.float32
        )
        for i in range(a // NB, min(a + wide, width) // NB):
            for j in range(i, width // NB):
                at = place[i, j] * NB
                acc[at : at + NB, :] += piece[i * NB - a : i * NB - a + NB, j * NB - a : j * NB - a + NB]


def gram_kernel(count, shards, last, place_ref, *rest):
    xs, rest = rest[:count], rest[count:]
    gates, rest = rest[:shards], rest[shards:]
    ups, rest = rest[:shards], rest[shards:]
    if last:
        before, rest = rest[0], rest[1:]
        sent, kept, rows_v, w_v, acc, x_sem, w_sem, a_sem = rest
    else:
        acc, rows_v, w_v, x_sem, w_sem = rest
    depth, width = gates[0].shape
    loads = []
    for s in range(shards):
        at = pl.ds(pl.multiple_of(place_ref[2 + s] * depth, depth), depth)
        loads.append(pltpu.make_async_copy(gates[s], w_v.at[at, pl.ds(0, width)], w_sem.at[2 * s]))
        loads.append(pltpu.make_async_copy(ups[s], w_v.at[at, pl.ds(width, width)], w_sem.at[2 * s + 1]))
    at = 0
    for k, x in enumerate(xs):
        loads.append(pltpu.make_async_copy(x, rows_v.at[pl.ds(at, x.shape[0]), :], x_sem.at[k]))
        at += x.shape[0]
    if last:
        loads.append(pltpu.make_async_copy(before, acc, a_sem))
    for load in loads:
        load.start()
    if not last:
        acc[...] = jnp.zeros(acc.shape, acc.dtype)
    for load in loads:
        load.wait()
    tile = 2 * BROWS

    def step(t, carry):
        x = rows_v[pl.ds(pl.multiple_of(t * tile, tile), tile), :]
        gate = jnp.dot(x, w_v[:, :width], preferred_element_type=jnp.float32)
        lifted = jnp.dot(x, w_v[:, width:], preferred_element_type=jnp.float32)
        hidden = gate / (1.0 + jnp.exp(-gate)) * lifted
        add_gram(acc, hidden)
        return carry

    lax.fori_loop(0, at // tile, step, 0)
    if last:
        half = sent.shape[0]
        mine = place_ref[0]
        kept[...] = acc[pl.ds(pl.multiple_of(mine * half, 8), half), :]
        sent[...] = acc[pl.ds(pl.multiple_of((1 - mine) * half, 8), half), :]


def gram_call(xs, gates, ups, before, place):
    last = before is not None
    depth, width = gates[0].shape
    shards = len(gates)
    rows = sum(x.shape[0] for x in xs)
    model = xs[0].shape[1]
    packed = len(upper_blocks(width)) * NB
    anywhere = pl.BlockSpec(memory_space=pl.ANY)
    vmem = pl.BlockSpec(memory_space=pltpu.VMEM)
    smem = pl.BlockSpec(memory_space=pltpu.SMEM)
    scratch = [
        pltpu.VMEM((rows, model), jnp.bfloat16),
        pltpu.VMEM((model, 2 * width), jnp.bfloat16),
    ]
    sems = [pltpu.SemaphoreType.DMA((len(xs),)), pltpu.SemaphoreType.DMA((2 * shards,))]
    whole = jax.ShapeDtypeStruct((packed, NB), jnp.float32)
    half = jax.ShapeDtypeStruct((packed // 2, NB), jnp.float32)
    if last:
        scratch = scratch + [pltpu.VMEM((packed, NB), jnp.float32)] + sems + [pltpu.SemaphoreType.DMA]
    else:
        scratch = scratch + sems
    return pl.pallas_call(
        functools.partial(gram_kernel, len(xs), shards, last),
        out_shape=[half, half] if last else whole,
        in_specs=[smem] + [anywhere] * (len(xs) + 2 * shards + last),
        out_specs=[vmem, vmem] if last else vmem,
        scratch_shapes=scratch,
        cost_estimate=pl.CostEstimate(
            flops=2 * rows * width * (2 * model + 2 * width),
            bytes_accessed=2 * (rows * model + 2 * model * width),
            transcendentals=rows * width,
        ),
        name="gram_last" if last else "gram_first",
    )(place, *xs, *gates, *ups, *([before] if last else []))


def combine_kernel(bit, place_ref, kept_ref, got_ref, *outs):
    half = outs[0].shape[0]
    if len(outs) == 1:
        outs[0][...] = kept_ref[...] + got_ref[...]
        return
    mine = (place_ref[1] >> bit) & 1
    for out, which in zip(outs, (1 - mine, mine)):
        at = pl.ds(pl.multiple_of(which * half, 8), half)
        out[...] = kept_ref[at, :] + got_ref[at, :]


def combine(kept, got, place, bit):
    rows = kept.shape[0]
    vmem = pl.BlockSpec(memory_space=pltpu.VMEM)
    parts = 1 if bit is None else 2
    out = jax.ShapeDtypeStruct((rows // parts, NB), jnp.float32)
    return pl.pallas_call(
        functools.partial(combine_kernel, bit),
        out_shape=[out] * parts,
        in_specs=[pl.BlockSpec(memory_space=pltpu.SMEM), vmem, vmem],
        out_specs=[vmem] * parts,
        name="combine",
    )(place, kept, got)


def factor_kernel(rows_avg, masks, place_ref, *rest):
    pieces, rest = rest[: len(masks)], rest[len(masks) :]
    down_ref, mine_ref, product_ref, packed, work, inverse = rest
    width = work.shape[0]
    my_rows = mine_ref.shape[0]
    count = width // NB
    sub = lax.broadcasted_iota(jnp.int32, (8, NB), 0)
    lane = lax.broadcasted_iota(jnp.int32, (8, NB), 1)
    share = pieces[0].shape[0]
    bits = len(masks).bit_length() - 1
    me = place_ref[1]
    slot = jnp.int32(0)
    for b in range(bits):
        slot = slot * 2 + ((me >> b) & 1)
    for mask, piece in zip(masks, pieces):
        turned = sum(((mask >> b) & 1) << (bits - 1 - b) for b in range(bits))
        packed[pl.ds(pl.multiple_of((slot ^ turned) * share, 8), share), :] = piece[...]
    big_sub = lax.broadcasted_iota(jnp.int32, (NB, NB), 0)
    big_lane = lax.broadcasted_iota(jnp.int32, (NB, NB), 1)
    for (i, j), at in upper_blocks(width).items():
        block = packed[at * NB : at * NB + NB, :] / float(rows_avg)
        if i == j:
            block = block + jnp.where(big_sub == big_lane, damping, 0.0)
        else:
            work[j * NB : j * NB + NB, i * NB : i * NB + NB] = jnp.zeros((NB, NB), jnp.float32)
        work[i * NB : i * NB + NB, j * NB : j * NB + NB] = block

    def step(kb, carry):
        off = pl.multiple_of(kb * NB, NB)
        rows = [work[pl.ds(off + 8 * i, 8), pl.ds(off, NB)] for i in range(NB // 8)]
        upper, low_inv = factor_block(rows)
        for i in range(NB // 8):
            work[pl.ds(off + 8 * i, 8), pl.ds(off, NB)] = jnp.where(lane >= sub + 8 * i, upper[i], 0.0)
            inverse[8 * i : 8 * i + 8, :] = low_inv[i]
        for k in range(count):
            @pl.when(kb == k)
            def _():
                at, lo = k * NB, (k + 1) * NB
                if k < count - 1:
                    panel = jnp.dot(
                        inverse[...], work[at:lo, lo:], precision=HIGHEST, preferred_element_type=jnp.float32
                    )
                    work[at:lo, lo:] = panel
                    for i in range(k + 1, count):
                        a = i * NB
                        work[a : a + NB, a:] -= lax.dot_general(
                            panel[:, a - lo : a - lo + NB],
                            panel[:, a - lo :],
                            (((0,), (0,)), ((), ())),
                            precision=HIGHEST,
                            preferred_element_type=jnp.float32,
                        )
                down = down_ref[at:, :]
                parts = [
                    jnp.dot(piece, down, preferred_element_type=jnp.float32)
                    for piece in split3(work[at:lo, at:])
                ]
                product_ref[at:lo, :] = parts[0] + (parts[1] + parts[2])
        return carry

    lax.fori_loop(0, count, step, 0)
    start = pl.multiple_of(place_ref[1] * my_rows, 8)
    mine_ref[...] = work[pl.ds(start, my_rows), :]


def factor_and_product(pieces, masks, down, place, rows_avg, my_rows):
    width = down.shape[0]
    vmem = pl.BlockSpec(memory_space=pltpu.VMEM)
    return pl.pallas_call(
        functools.partial(factor_kernel, rows_avg, masks),
        out_shape=(
            jax.ShapeDtypeStruct((my_rows, width), jnp.float32),
            jax.ShapeDtypeStruct((width, down.shape[1]), jnp.float32),
        ),
        in_specs=[pl.BlockSpec(memory_space=pltpu.SMEM)] + [vmem] * (len(masks) + 1),
        out_specs=(vmem, vmem),
        scratch_shapes=[
            pltpu.VMEM((pieces[0].shape[0] * len(masks), NB), jnp.float32),
            pltpu.VMEM((width, width), jnp.float32),
            pltpu.VMEM((NB, NB), jnp.float32),
        ],
        name="factor",
    )(place, *pieces, down)


def on_device(tokens, block_expert, gate_weight, up_weight, down_weight):
    n_expert = lax.axis_size("expert")
    n_data = lax.axis_size("dp")
    width = gate_weight.shape[2]
    blk_count = block_expert.shape[0]
    experts = gate_weight.shape[0] * n_expert
    capacity = max(2, 2 * blk_count // experts)
    rows_avg = blk_count * BROWS * n_data * n_expert // experts
    bits = n_data.bit_length() - 1
    inner = 1 << (bits // 2)
    outer = n_data // inner
    e = lax.axis_index("expert").astype(jnp.int32)
    d = lax.axis_index("dp").astype(jnp.int32)

    def swap_expert(x, offset):
        return lax.ppermute(x, "expert", [(k, k ^ offset) for k in range(n_expert)])

    def swap_data(x, mask):
        return lax.ppermute(x, "dp", [(k, k ^ mask) for k in range(n_data)])

    def turn(x, o, i):
        moved = [(k, (k // inner + o) % outer * inner + (k % inner + i) % inner) for k in range(n_data)]
        return lax.ppermute(x, "dp", moved)

    far = list(range(2, n_expert))
    head = capacity - 1
    me = e.reshape(1)
    first = dispatch(tokens, block_expert, me, [(o, 0, head) for o in far] + [(o, head, 1) for o in far])
    near = dispatch(tokens, block_expert, me, [(1, 0, capacity), (0, 0, capacity)])
    early = [swap_expert(x, o) for x, o in zip(first[: len(far)], far)]
    late = [swap_expert(x, o) for x, o in zip(first[len(far) :], far)]
    beside = swap_expert(near[0], 1)

    held = {}
    for name, weight in (("gate", gate_weight[0]), ("up", up_weight[0])):
        held[name, 0, 0] = weight
    for o in range(outer):
        for name in ("gate", "up"):
            if o:
                held[name, o, 0] = turn(held[name, o - 1, 0], 1, 0)
        for i in range(1, inner):
            for name in ("gate", "up"):
                held[name, o, i] = turn(held[name, o, i - 1], 0, 1)
    keys = [(o, i) for o in range(outer) for i in range(inner)]
    owners = [(d // inner - o + outer) % outer * inner + (d % inner - i + inner) % inner for o, i in keys]
    place = jnp.stack([d & 1, d] + owners).astype(jnp.int32)
    gates = [held[("gate",) + k] for k in keys]
    ups = [held[("up",) + k] for k in keys]

    before = gram_call([near[1], beside] + early, gates, ups, None, place)
    sent, kept = gram_call(late, gates, ups, before, place)

    for b in range(bits):
        got = swap_data(sent, 1 << b)
        if b + 1 < bits:
            sent, kept = combine(kept, got, place, b + 1)
        else:
            (share,) = combine(kept, got, place, None)
    shares = {0: share}
    for b in reversed(range(bits)):
        for mask in sorted(shares):
            shares[mask | (1 << b)] = swap_data(shares[mask], 1 << b)
    masks = sorted(shares)
    mine, product = factor_and_product(
        [shares[m] for m in masks], masks, down_weight[0], place, rows_avg, width // n_data
    )
    return (mine[None], product[None])


def solution(mesh):
    placed = (
        P(("expert", "dp"), None),
        P(("expert", "dp"), None),
        P("expert", "dp", None),
        P("expert", "dp", None),
        P("expert", None, "dp"),
    )
    return jax.shard_map(
        on_device,
        mesh=mesh,
        in_specs=placed,
        out_specs=(P("expert", "dp", None), P("expert", None, "dp")),
        check_vma=False,
    )
```
